128 devices in a mesh: pb: 16 (over z, y), pa: 8 (over x, core).
Axes of the slice: x: 4, y: 4, z: 4, core: 2. Of those that a mesh axis runs over, the one named last changes fastest.
Arguments:
- queries: float32 [16384, 4096], P('pb'), may hold values from -2.0898438 to 2.0898438
- passages: float32 [2048, 4096], P('pa', 'pb'), may hold values from -0.15625 to 0.15625
- pairs: int32 [384, 2], P('pb'), may hold values from 0 to 63, as said below
- positives: int32 [16384], P('pb'), may hold values from 0 to 2047, as said below
Outputs:
- losses: float32 [16384], P('pb')
- query_grad: float32 [16384, 4096], P('pb', 'pa')
- passage_grad: float32 [2048, 4096], P('pa', 'pb')
The draws below stay inside these ranges and needn't reach their ends.
Inputs may be any that keep to these rules, and one draw needn't show every extreme that they name: Rows k * 24 to (k + 1) * 24 - 1 list query blocks k * 4 to (k + 1) * 4 - 1 only, in column 0; column 1 holds passage blocks. No pair appears twice and every query block appears in at least one pair; the number of pairs of a query block varies. The passage block of positives[i], positives[i] // 256, is listed with the query block of i.
All inputs are finite; a program needn't handle non-finite values.
Results may differ from the reference program's by a relative error of at most 0.0008.
Values sent between devices are 32-bit elements; how exact they have to be, the bound alone decides.
No kernel may reach another device: no remote copies, remote signals or barrier semaphores. Data moves between devices by JAX's collectives and lax.ppermute only.
A program may use at most 192 MiB of HBM per device.

```python
import math
import jax
import jax.numpy as jnp
from jax import lax

D = 4096
BLK = 256
QB_DEV = 4
DOC_TILES_SHARE = 1
QBLOCKS = 64
DOCUMENT_TILES = 8
NQ = 16384
NP = 2048
PAIRS_DEV = 24


def layout(key):
    owners = QBLOCKS // QB_DEV
    groups = DOCUMENT_TILES // DOC_TILES_SHARE
    key_rank, key_noise, key_home, key_offset = jax.random.split(jax.random.fold_in(key, 11), 4)
    sorted_indices = jax.random.permutation(key_rank, groups).astype(jnp.int32)
    reward_table = sorted_indices[jnp.arange(DOCUMENT_TILES, dtype=jnp.int32) // DOC_TILES_SHARE] * 2048
    random_whole = jax.random.randint(key_noise, (owners, QB_DEV, DOCUMENT_TILES), 0, 16384, dtype=jnp.int32)
    home_flat = jax.random.randint(key_home, (QBLOCKS,), 0, DOCUMENT_TILES, dtype=jnp.int32)
    home_flat = home_flat.at[0].set(DOCUMENT_TILES - 1)
    home_flat = home_flat.at[QBLOCKS - 1].set(0)
    local_tiles = home_flat.reshape(owners, QB_DEV)
    tile_pairing = jnp.arange(DOCUMENT_TILES, dtype=jnp.int32)
    similarity_grid = jnp.where(tile_pairing[None, None, :] == local_tiles[:, :, None], 1 << 20, random_whole + reward_table[None, None, :])
    combos = jnp.arange(QB_DEV * DOCUMENT_TILES, dtype=jnp.int32)
    ranked = similarity_grid.reshape(owners, QB_DEV * DOCUMENT_TILES) * 1024 + combos[None, :]
    chosen = lax.top_k(ranked, PAIRS_DEV)[1].astype(jnp.int32)
    query_ids = jnp.arange(owners, dtype=jnp.int32)[:, None] * QB_DEV + chosen // DOCUMENT_TILES
    pair_list = jnp.stack([query_ids, chosen % DOCUMENT_TILES], axis=-1).reshape(owners * PAIRS_DEV, 2).astype(jnp.int32)
    offsets = jax.random.randint(key_offset, (QBLOCKS * BLK,), 0, BLK, dtype=jnp.int32)
    offsets = offsets.at[0].set(BLK - 1)
    offsets = offsets.at[QBLOCKS * BLK - 1].set(0)
    home_of_row = home_flat[jnp.arange(QBLOCKS * BLK, dtype=jnp.int32) // BLK]
    positive_ids = (home_of_row * BLK + offsets).astype(jnp.int32)
    return (pair_list, positive_ids)


def alignment(key):
    deviation = D ** (-0.5)
    key_pick, key_level = jax.random.split(jax.random.fold_in(key, 23), 2)
    selected = jax.random.randint(key_pick, (QBLOCKS * BLK,), 0, 64, dtype=jnp.int32) == 0
    selected = selected.at[0].set(True)
    level = jax.random.randint(key_level, (QBLOCKS * BLK,), 0, 3, dtype=jnp.int32)
    strength = jnp.where(level == 0, 110.0, jnp.where(level == 1, 180.0, 300.0)).astype(jnp.float32) * deviation
    return (selected, strength)


def partner_of(positive_ids):
    return positive_ids + 1 - 2 * (positive_ids % 2)


def draw_pairs(key, part):
    return layout(key)[0]


def draw_positives(key, part):
    return layout(key)[1]


def draw_passages(key, part):
    deviation = D ** (-0.5)
    key_base = jax.random.fold_in(jax.random.fold_in(key, 31), 0)
    base = jax.random.truncated_normal(key_base, -5.0, 5.0, (DOCUMENT_TILES * BLK, D), jnp.float32) * deviation
    return jnp.clip(base, -10.0 * deviation, 10.0 * deviation)


def draw_queries(key, part):
    deviation = D ** (-0.5)
    bound = 6000.0 / D + 40.0 * deviation
    key_base = jax.random.fold_in(jax.random.fold_in(key, 41), 0)
    base = jax.random.truncated_normal(key_base, -5.0, 5.0, (QBLOCKS * BLK, D), jnp.float32) * deviation
    passages_now = draw_passages(key, part)
    positive_ids = layout(key)[1]
    selected, strength = alignment(key)
    first_rows = passages_now[positive_ids]
    second_rows = passages_now[partner_of(positive_ids)]
    aligned_rows = strength[:, None] * first_rows + (strength - 2.0 * deviation)[:, None] * second_rows
    base = jnp.where(selected[:, None], aligned_rows, base)
    return jnp.clip(base, -bound, bound)


def setup_inputs(seed: int = 0) -> dict:
    key_list = jax.random.split(jax.random.key(seed), 5)
    return {
        "queries": draw_queries(jax.random.fold_in(key_list[4], 71), 0),
        "passages": draw_passages(jax.random.fold_in(key_list[4], 71), 0),
        "pairs": draw_pairs(jax.random.fold_in(key_list[4], 71), 0),
        "positives": draw_positives(jax.random.fold_in(key_list[4], 71), 0),
    }


low_value = -1e+30
highest = lax.Precision.HIGHEST

def reference(queries, passages, pairs, positives):
    inv_temp = math.sqrt(D)
    columns = jnp.arange(BLK, dtype=jnp.int32)

    def blocks_for(pair_now):
        query_block = lax.dynamic_slice_in_dim(queries, (pair_now[0] * BLK).astype(jnp.int32), BLK, 0)
        passage_block = lax.dynamic_slice_in_dim(passages, (pair_now[1] * BLK).astype(jnp.int32), BLK, 0)
        wanted = lax.dynamic_slice_in_dim(positives, (pair_now[0] * BLK).astype(jnp.int32), BLK, 0) - pair_now[1] * BLK
        hits = columns[None, :] == wanted[:, None]
        return (query_block, passage_block, hits)

    def forward(running, pair_now):
        row_max, row_sum, pos_score = running
        parts_now = blocks_for(pair_now)
        similarity_grid = inv_temp * lax.dot_general(parts_now[0], parts_now[1], (((1,), (1,)), ((), ())), precision=highest, preferred_element_type=jnp.float32)
        start_row = (pair_now[0] * BLK).astype(jnp.int32)
        previous = lax.dynamic_slice_in_dim(row_max, start_row, BLK, 0)
        new_max = jnp.maximum(previous, lax.optimization_barrier(jnp.max(similarity_grid, axis=1)))
        old_sum = lax.dynamic_slice_in_dim(row_sum, start_row, BLK, 0)
        new_sum = old_sum * jnp.exp(previous - new_max) + lax.optimization_barrier(jnp.sum(jnp.exp(similarity_grid - new_max[:, None]), axis=1))
        old_pos = lax.dynamic_slice_in_dim(pos_score, start_row, BLK, 0)
        new_pos = old_pos + lax.optimization_barrier(jnp.sum(jnp.where(parts_now[2], similarity_grid, jnp.zeros_like(similarity_grid)), axis=1))
        row_max = lax.dynamic_update_slice_in_dim(row_max, new_max, start_row, 0)
        row_sum = lax.dynamic_update_slice_in_dim(row_sum, new_sum, start_row, 0)
        pos_score = lax.dynamic_update_slice_in_dim(pos_score, new_pos, start_row, 0)
        return ((row_max, row_sum, pos_score), similarity_grid)
    initial = (jnp.full((NQ,), low_value, jnp.float32), jnp.zeros((NQ,), jnp.float32), jnp.zeros((NQ,), jnp.float32))
    stats, all_tiles = lax.scan(forward, initial, pairs)
    log_norm = stats[0] + jnp.log(stats[1])
    losses = log_norm - stats[2]

    def backward(running, inputs):
        query_grad, passage_grad = running
        pair_now, similarity_grid = inputs
        parts_now = blocks_for(pair_now)
        start_row = (pair_now[0] * BLK).astype(jnp.int32)
        start_col = (pair_now[1] * BLK).astype(jnp.int32)
        norm_rows = lax.dynamic_slice_in_dim(log_norm, start_row, BLK, 0)
        weights = jnp.exp(similarity_grid - norm_rows[:, None]) - parts_now[2].astype(jnp.float32)
        query_term = inv_temp * jnp.dot(weights, parts_now[1], precision=highest, preferred_element_type=jnp.float32)
        passage_term = inv_temp * lax.dot_general(weights, parts_now[0], (((0,), (0,)), ((), ())), precision=highest, preferred_element_type=jnp.float32)
        old_query = lax.dynamic_slice_in_dim(query_grad, start_row, BLK, 0)
        old_passage = lax.dynamic_slice_in_dim(passage_grad, start_col, BLK, 0)
        query_grad = lax.dynamic_update_slice_in_dim(query_grad, old_query + query_term, start_row, 0)
        passage_grad = lax.dynamic_update_slice_in_dim(passage_grad, old_passage + passage_term, start_col, 0)
        return ((query_grad, passage_grad), None)
    grads_init = (jnp.zeros((NQ, D), jnp.float32), jnp.zeros((NP, D), jnp.float32))
    grads, unused = lax.scan(backward, grads_init, (pairs, all_tiles))
    return (losses, grads[0], grads[1])
```

```python
import jax
import jax.numpy as jnp
from jax import lax
from jax.experimental import pallas as pl
from jax.experimental.pallas import tpu as pltpu
from jax.sharding import PartitionSpec as P

BLK = 256
HALF = 128
ROWS = 1024
SCALE = 64.0
LOW = -1e30
MIB = 1 << 20


def along_x(d):
    return [(x * 2 + c, (x + d) % 4 * 2 + c) for x in range(4) for c in range(2)]


def along_y(d):
    return [(z * 4 + y, z * 4 + (y + d) % 4) for z in range(4) for y in range(4)]


def along_z(d):
    return [(z * 4 + y, (z + d) % 4 * 4 + y) for z in range(4) for y in range(4)]


SWAP = [(x * 2 + c, x * 2 + 1 - c) for x in range(4) for c in range(2)]


def turned():
    moves = []
    for z in range(4):
        for y in range(4):
            for x in range(4):
                for c in range(2):
                    source = (z * 4 + y) * 8 + x * 2 + c
                    target = (x * 4 + 2 * (y % 2) + c) * 8 + z * 2 + y // 2
                    moves.append((source, target))
    return moves


def ring(own, axis, along):
    after = lax.ppermute(own, axis, along(-1))
    before = lax.ppermute(own, axis, along(1))
    far = lax.ppermute(own, axis, along(2))
    return jnp.stack([own, after, far, before])


def gathered(block):
    top, low = block[:HALF], block[HALF:]
    top, low = ring(top, "pb", along_y), ring(low, "pb", along_z)
    return ring(top, "pb", along_z), ring(low, "pb", along_y)


def summed(parts, axis, along):
    arrived = [lax.ppermute(parts[d], axis, along(d)) for d in (1, 3, 2)]
    return parts[0] + arrived[0] + (arrived[1] + arrived[2])


def split2(value):
    high = value.astype(jnp.bfloat16)
    return high, (value - high.astype(jnp.float32)).astype(jnp.bfloat16)


def score_kernel(at, q_ref, top_ref, low_ref, out_ref):
    step = pl.program_id(0)
    block = jnp.concatenate([top_ref[0, 0], low_ref[0, 0]], axis=0)
    product = lax.dot_general(
        q_ref[...],
        block,
        (((1,), (1,)), ((), ())),
        precision=lax.Precision.HIGHEST,
        preferred_element_type=jnp.float32,
    )

    @pl.when(step == 0)
    def _():
        out_ref[...] = SCALE * product

    @pl.when(step > 0)
    def _():
        out_ref[...] += SCALE * product


def feature_block(step, at):
    return (at[0] + step // 4) % 4 * 4 + (at[1] + step % 4) % 4


def scores_of(at, queries, top, low):
    spec = pltpu.PrefetchScalarGridSpec(
        num_scalar_prefetch=1,
        grid=(16,),
        in_specs=[
            pl.BlockSpec((ROWS, BLK), lambda i, at: (0, feature_block(i, at))),
            pl.BlockSpec((1, 1, HALF, BLK), lambda i, at: (i // 4, i % 4, 0, 0)),
            pl.BlockSpec((1, 1, HALF, BLK), lambda i, at: (i % 4, i // 4, 0, 0)),
        ],
        out_specs=pl.BlockSpec((ROWS, BLK), lambda i, at: (0, 0)),
    )
    return pl.pallas_call(
        score_kernel,
        grid_spec=spec,
        out_shape=jax.ShapeDtypeStruct((ROWS, BLK), jnp.float32),
        name="scores",
    )(at, queries, top, low)


def group_of(at, side, dx):
    core = at[3] if side == 0 else 1 - at[3]
    return (at[2] + dx) % 4 * 2 + core


def masked(tile, live):
    return jnp.where(live > 0, tile, LOW)


def passage_kernel(
    at, live, q_ref, same_ref, other_ref, pos_ref, top_ref, low_ref, loss_ref, norm_ref, wt_ref
):
    step = pl.program_id(0)

    @pl.when(step == 0)
    def _():
        columns = lax.broadcasted_iota(jnp.int32, (HALF, BLK), 1)

        def chunk(r, carry):
            rows = pl.ds(pl.multiple_of(r * HALF, HALF), HALF)
            block = r // 2
            wanted = pos_ref[rows, :]
            tiles = []
            for side, ref in ((0, same_ref), (1, other_ref)):
                for dx in range(4):
                    group = group_of(at, side, dx)
                    hit = columns == wanted - group * BLK
                    tiles.append((masked(ref[dx, rows, :], live[block * 8 + group]), hit))
            top = tiles[0][0]
            for tile, _ in tiles[1:]:
                top = jnp.maximum(top, tile)
            row_max = jnp.max(top, axis=1, keepdims=True)
            total = jnp.exp(tiles[0][0] - row_max)
            found = jnp.where(tiles[0][1], tiles[0][0], 0.0)
            for tile, hit in tiles[1:]:
                total += jnp.exp(tile - row_max)
                found += jnp.where(hit, tile, 0.0)
            norm = row_max + jnp.log(jnp.sum(total, axis=1, keepdims=True))
            loss_ref[rows, :] = norm - jnp.sum(found, axis=1, keepdims=True)
            norm_ref[rows, :] = norm
            tile, hit = tiles[0]
            weight = SCALE * (jnp.exp(tile - norm) - hit.astype(jnp.float32))
            high, low = split2(weight.T)
            wt_ref[:, pl.ds(pl.multiple_of(r * HALF, HALF), HALF)] = high
            wt_ref[:, pl.ds(pl.multiple_of(ROWS + r * HALF, HALF), HALF)] = high
            wt_ref[:, pl.ds(pl.multiple_of(2 * ROWS + r * HALF, HALF), HALF)] = low
            return carry

        lax.fori_loop(0, ROWS // HALF, chunk, 0)

    high, low = split2(q_ref[...])
    product = jnp.dot(
        wt_ref[...],
        jnp.concatenate([high, low, high], axis=0),
        preferred_element_type=jnp.float32,
    )
    top_ref[0, 0] = product[:HALF]
    low_ref[0, 0] = product[HALF:]


def passage_parts(at, live, queries, same, other, wanted):
    whole = pl.BlockSpec(memory_space=pltpu.VMEM)
    column = pl.BlockSpec((ROWS, 1), lambda i, at, live: (0, 0))
    spec = pltpu.PrefetchScalarGridSpec(
        num_scalar_prefetch=2,
        grid=(16,),
        in_specs=[
            pl.BlockSpec((ROWS, BLK), lambda i, at, live: (0, feature_block(i, at))),
            whole,
            whole,
            whole,
        ],
        out_specs=[
            pl.BlockSpec((1, 1, HALF, BLK), lambda i, at, live: (i // 4, i % 4, 0, 0)),
            pl.BlockSpec((1, 1, HALF, BLK), lambda i, at, live: (i % 4, i // 4, 0, 0)),
            column,
            column,
        ],
        scratch_shapes=[pltpu.VMEM((BLK, 3 * ROWS), jnp.bfloat16)],
    )
    part = jax.ShapeDtypeStruct((4, 4, HALF, BLK), jnp.float32)
    line = jax.ShapeDtypeStruct((ROWS, 1), jnp.float32)
    return pl.pallas_call(
        passage_kernel,
        grid_spec=spec,
        out_shape=[part, part, line, line],
        name="passage_parts",
    )(at, live, queries, same, other, wanted)


def query_kernel(at, live, same_ref, other_ref, pos_ref, norm_ref, top_ref, low_ref, out_ref):
    dx = pl.program_id(0)
    columns = lax.broadcasted_iota(jnp.int32, (BLK, BLK), 1)
    for side, ref in ((0, same_ref), (1, other_ref)):
        group = group_of(at, side, dx)
        x, core = group // 2, group % 2
        dz = (x - at[0] + 4) % 4
        blocks = []
        for h in range(2):
            dy = (2 * h + core - at[1] + 4) % 4
            blocks.append(jnp.concatenate([top_ref[dz, dy], low_ref[dy, dz]], axis=0))
        high, low = split2(jnp.concatenate(blocks, axis=1))
        passages = jnp.concatenate([high, low, high], axis=0)
        for block in range(4):
            rows = pl.ds(block * BLK, BLK)
            tile = masked(ref[0, rows, :], live[block * 8 + group])
            hit = columns == pos_ref[rows, :] - group * BLK
            weight = SCALE * (jnp.exp(tile - norm_ref[rows, :]) - hit.astype(jnp.float32))
            high, low = split2(weight)
            product = jnp.dot(
                jnp.concatenate([high, high, low], axis=1),
                passages,
                preferred_element_type=jnp.float32,
            )
            if side:
                out_ref[rows, :] += product
            else:

                @pl.when(dx == 0)
                def _():
                    out_ref[rows, :] = product

                @pl.when(dx > 0)
                def _():
                    out_ref[rows, :] += product


def query_gradient(at, live, same, other, wanted, norm, top, low):
    whole = pl.BlockSpec(memory_space=pltpu.VMEM)
    tile = pl.BlockSpec((1, ROWS, BLK), lambda i, at, live: (i, 0, 0))
    spec = pltpu.PrefetchScalarGridSpec(
        num_scalar_prefetch=2,
        grid=(4,),
        in_specs=[tile, tile, whole, whole, whole, whole],
        out_specs=pl.BlockSpec((ROWS, 2 * BLK), lambda i, at, live: (0, 0)),
    )
    return pl.pallas_call(
        query_kernel,
        grid_spec=spec,
        out_shape=jax.ShapeDtypeStruct((ROWS, 2 * BLK), jnp.float32),
        name="query_gradient",
    )(at, live, same, other, wanted, norm, top, low)


def body(queries, passages, pairs, positives):
    owner, group = lax.axis_index("pb"), lax.axis_index("pa")
    at = jnp.stack([owner // 4, owner % 4, group // 2, group % 2]).astype(jnp.int32)
    cells = jnp.arange(32, dtype=jnp.int32)
    listed = (pairs[:, 0] - owner * 4) * 8 + pairs[:, 1]
    live = jnp.any(cells[:, None] == listed[None, :], axis=1).astype(jnp.int32)
    wanted = positives.reshape(ROWS, 1)

    top, low = gathered(passages)
    tile = scores_of(at, queries, top, low)
    turned_block = lax.ppermute(passages, ("pb", "pa"), turned())
    top2, low2 = gathered(turned_block)
    same = ring(tile, "pa", along_x)
    other = lax.ppermute(same, "pa", SWAP)
    part_top, part_low, losses, norm = passage_parts(at, live, queries, same, other, wanted)
    query_grad = query_gradient(at, live, same, other, wanted, norm, top2, low2)
    part_top = summed(part_top, "pb", along_z)
    part_low = summed(part_low, "pb", along_y)
    part_top = summed(part_top, "pb", along_y)
    part_low = summed(part_low, "pb", along_z)
    passage_grad = jnp.concatenate([part_top, part_low], axis=0)
    return (losses.reshape(ROWS), query_grad, passage_grad)


def solution(mesh):
    in_specs = (P("pb", None), P("pa", "pb"), P("pb", None), P("pb"))
    out_specs = (P("pb"), P("pb", "pa"), P("pa", "pb"))
    return jax.shard_map(body, mesh=mesh, in_specs=in_specs, out_specs=out_specs, check_vma=False)
```
